32 devices in a mesh: dp: 8 (over z, core), tensor: 4 (over y, x).
Axes of the slice: x: 2, y: 2, z: 4, core: 2. Of those that a mesh axis runs over, the one named last changes fastest.
Arguments:
- inputs: bfloat16 [2048, 2048], P('dp'), may hold values from -6 to 6
- first_gain: float32 [2048], replicated, may hold values from 0.1 to 1.9
- first_shift: float32 [2048], replicated, may hold values from -2 to 2
- query_weight: bfloat16 [2048, 2048], P(None, 'tensor'), may hold values from -0.125 to 0.125
- key_weight: bfloat16 [2048, 2048], P(None, 'tensor'), may hold values from -0.125 to 0.125
- value_weight: bfloat16 [2048, 4096], P(None, 'tensor'), may hold values from -0.125 to 0.125
- gate_weight: bfloat16 [2048, 4096], P(None, 'tensor'), may hold values from -0.125 to 0.125
- output_weight: bfloat16 [4096, 2048], P('tensor'), may hold values from -0.25 to 0.25
- second_gain: float32 [2048], replicated, may hold values from 0.1 to 1.9
- second_shift: float32 [2048], replicated, may hold values from -2 to 2
- inner_weight: bfloat16 [2048, 4096], P(None, 'tensor'), may hold values from -0.125 to 0.125
- inner_bias: float32 [4096], P('tensor'), may hold values from -3 to 3
- outer_weight: bfloat16 [4096, 2048], P('tensor'), may hold values from -0.1875 to 0.1875
- outer_bias: float32 [2048], replicated, may hold values from -3 to 3
- cotangent: bfloat16 [2048, 2048], P('dp'), may hold values from -6 to 6
- lengths: int32 [32], replicated, may hold values from 1 to 253, as said below
- owners: int32 [32], replicated, may hold values from 0 to 7, as said below
- offsets: int32 [32], replicated, may hold values from 0 to 255, as said below
Outputs:
- outputs: bfloat16 [2048, 2048], P('dp')
- input_grad: float32 [2048, 2048], P('dp')
- first_gain_grad: float32 [2048], replicated
- first_shift_grad: float32 [2048], replicated
- query_weight_grad: float32 [2048, 2048], P(None, 'tensor')
- key_weight_grad: float32 [2048, 2048], P(None, 'tensor')
- value_weight_grad: float32 [2048, 4096], P(None, 'tensor')
- gate_weight_grad: float32 [2048, 4096], P(None, 'tensor')
- output_weight_grad: float32 [4096, 2048], P('tensor')
- second_gain_grad: float32 [2048], replicated
- second_shift_grad: float32 [2048], replicated
- inner_weight_grad: float32 [2048, 4096], P(None, 'tensor')
- inner_bias_grad: float32 [4096], P('tensor')
- outer_weight_grad: float32 [4096, 2048], P('tensor')
- outer_bias_grad: float32 [2048], replicated
The draws below stay inside these ranges and needn't reach their ends.
Inputs may be any that keep to these rules, and one draw needn't show every extreme that they name: `lengths`: within one index of dp its sequences lie end to end from slot 0 in increasing offsets; they fill between a quarter of its 256 slots and all of them, the slots after the last sequence are unused, and some index is full in every draw. `owners`: every index of dp holds exactly 4 sequences. offsets[j] is the sum of the lengths of the sequences of the same owner that lie before sequence j.
All inputs are finite; a program needn't handle non-finite values.
Results may differ from the reference program's by a relative error of at most 0.02.
Values may be sent and summed in bfloat16 or wider, within the bound.
No kernel may reach another device: no remote copies, remote signals or barrier semaphores. Data moves between devices by JAX's collectives and lax.ppermute only.
A program may use at most 320 MiB of HBM per device.

```python
import jax
import jax.numpy as jnp
from jax import lax

D = 2048
HEADS = 8
DK = 256
DV = 512
FF = 4096
TOKEN_SLOTS_EACH = 256
SEQ_DEV = 4
TOKENS = 2048
N_DP = 8
N_TENSOR = 4


def dealing(key):
    base = jax.random.fold_in(key, 31)
    order_key, fill_key, cut_key, full_key, second_key = jax.random.split(base, 5)
    groups = jnp.arange(N_DP, dtype=jnp.int32)
    fills = jax.random.randint(fill_key, (N_DP,), TOKEN_SLOTS_EACH // 4, TOKEN_SLOTS_EACH + 1)
    chosen = jax.random.randint(full_key, (), 0, N_DP)
    second = (chosen + 1 + jax.random.randint(second_key, (), 0, N_DP - 1)) % N_DP
    fills = jnp.where(groups == chosen, TOKEN_SLOTS_EACH, fills)
    fills = jnp.where(groups == second, TOKEN_SLOTS_EACH, fills)
    cuts = jax.random.randint(cut_key, (N_DP, SEQ_DEV - 1), 0, (fills - SEQ_DEV + 1)[:, None])
    cuts = jnp.sort(cuts, axis=1)
    last_cut = jnp.where(groups == second, fills - SEQ_DEV, cuts[:, -1])
    cuts = jnp.concatenate([cuts[:, :-1], last_cut[:, None]], axis=1)
    cuts = jnp.where((groups == chosen)[:, None], 0, cuts)
    bounds = jnp.concatenate([jnp.zeros((N_DP, 1), jnp.int32), cuts.astype(jnp.int32), (fills - SEQ_DEV)[:, None].astype(jnp.int32)], axis=1)
    spans = bounds[:, 1:] - bounds[:, :-1] + 1
    firsts = jnp.concatenate([jnp.zeros((N_DP, 1), jnp.int32), jnp.cumsum(spans, axis=1)[:, :-1].astype(jnp.int32)], axis=1)
    order = jax.random.permutation(order_key, N_DP * SEQ_DEV).astype(jnp.int32)
    owner = order // SEQ_DEV
    rank = order % SEQ_DEV
    return (spans[owner, rank].astype(jnp.int32), owner.astype(jnp.int32), firsts[owner, rank].astype(jnp.int32))


def draw_lengths(key, part):
    return dealing(key)[0]


def draw_owners(key, part):
    return dealing(key)[1]


def draw_offsets(key, part):
    return dealing(key)[2]


def block_levels(key, dims, shards, low, high):
    loudness = 1.0
    for position, shards_of in shards:
        steps = jax.random.uniform(jax.random.fold_in(jax.random.fold_in(key, 6), position), (shards_of,), jnp.float32, low / len(shards), high / len(shards))
        loudness = loudness * jnp.repeat(jnp.exp(steps), dims[position] // shards_of).reshape((-1,) + (1,) * (len(dims) - 1 - position))
    return loudness


def centred(stream_key, shape, deviation, reach, pieces=(), kind=jnp.bfloat16):
    entries = jax.random.normal(stream_key, shape, jnp.float32) * deviation
    if len(pieces) > 0:
        entries = block_levels(stream_key, shape, pieces, -0.22, 0.18) * entries
    return jnp.clip(entries, min=-reach, max=reach).astype(kind)


def setup_inputs(seed: int = 0) -> dict:
    streams_of = jax.random.split(jax.random.key(seed), 19)
    inputs = centred(streams_of[0], (TOKENS, D), 1.0, 6.0, ((0, 8),))
    first_gain = jnp.clip(1.0 + 0.18 * jax.random.normal(streams_of[1], (D,), jnp.float32), 0.1, 1.9)
    first_shift = centred(streams_of[2], (D,), 0.3, 2.0, (), jnp.float32)
    query_weight = centred(streams_of[3], (D, HEADS * DK), D ** -0.5, 0.125, ((1, 4),))
    key_weight = centred(streams_of[4], (D, HEADS * DK), D ** -0.5, 0.125, ((1, 4),))
    value_weight = centred(streams_of[5], (D, HEADS * DV), D ** -0.5, 0.125, ((1, 4),))
    gate_weight = centred(streams_of[6], (D, HEADS * DV), D ** -0.5, 0.125, ((1, 4),))
    output_weight = centred(streams_of[7], (HEADS * DV, D), DV ** -0.5, 0.25, ((0, 4),))
    second_gain = jnp.clip(1.0 + 0.18 * jax.random.normal(streams_of[8], (D,), jnp.float32), 0.1, 1.9)
    second_shift = centred(streams_of[9], (D,), 0.3, 2.0, (), jnp.float32)
    inner_weight = centred(streams_of[10], (D, FF), D ** -0.5, 0.125, ((1, 4),))
    inner_bias = centred(streams_of[11], (FF,), 0.5, 3.0, ((0, 4),), jnp.float32)
    outer_weight = centred(streams_of[12], (FF, D), (FF // 4) ** -0.5, 0.1875, ((0, 4),))
    outer_bias = centred(streams_of[13], (D,), 0.5, 3.0, (), jnp.float32)
    cotangent = centred(streams_of[14], (TOKENS, D), 1.0, 6.0, ((0, 8),))
    lengths = draw_lengths(jax.random.fold_in(streams_of[18], 71), 0)
    owners = draw_owners(jax.random.fold_in(streams_of[18], 71), 0)
    offsets = draw_offsets(jax.random.fold_in(streams_of[18], 71), 0)
    return dict(inputs=inputs, first_gain=first_gain, first_shift=first_shift, query_weight=query_weight, key_weight=key_weight, value_weight=value_weight, gate_weight=gate_weight, output_weight=output_weight, second_gain=second_gain, second_shift=second_shift, inner_weight=inner_weight, inner_bias=inner_bias, outer_weight=outer_weight, outer_bias=outer_bias, cotangent=cotangent, lengths=lengths, owners=owners, offsets=offsets)


EPS = 1e-05
EXACT_GELU_MODE = lax.Precision.HIGHEST

def layer_norm(hidden, gain, shift):
    center = hidden - lax.optimization_barrier(jnp.mean(hidden, axis=-1, keepdims=True))
    spread = lax.optimization_barrier(jnp.mean(center * center, axis=-1, keepdims=True))
    return center * lax.rsqrt(spread + EPS) * gain + shift

def gelu_exact(value):
    return jax.nn.gelu(value, approximate=False)

def gate_norm(retained, gate):
    center = retained - lax.optimization_barrier(jnp.mean(retained, axis=-1, keepdims=True))
    spread = lax.optimization_barrier(jnp.mean(center * center, axis=-1, keepdims=True))
    scaled = (center * lax.rsqrt(spread + 1.0)).reshape(gate.shape)
    return jax.nn.silu(gate) * scaled

def head_decay(first_head, count):
    heads = (first_head + jnp.arange(count, dtype=jnp.int32)).astype(jnp.float32)
    return jnp.log1p(-jnp.exp2(-5.0 - heads))

def product(left, right):
    return jnp.dot(left, right, preferred_element_type=jnp.float32)

def retention_whole(query, keys, values, gate, starts, log_decay):
    rows = query.shape[0]
    heads = log_decay.shape[0]
    query_heads = query.reshape(rows, heads, -1)
    key_heads = keys.reshape(rows, heads, -1)
    value_heads = values.reshape(rows, heads, -1)
    slots = jnp.arange(rows, dtype=jnp.int32)
    live = (slots[None, :] <= slots[:, None]) & (slots[None, :] >= starts[:, None])
    distance = (slots[:, None] - slots[None, :]).astype(jnp.float32)
    power = jnp.where(live[None], distance[None] * log_decay[:, None, None], 0.0)
    weight = jnp.where(live[None], jnp.exp(power), 0.0)
    scores = jnp.einsum('nhk,mhk->hnm', query_heads, key_heads, precision=EXACT_GELU_MODE) * weight
    retained = jnp.einsum('hnm,mhv->nhv', scores, value_heads, precision=EXACT_GELU_MODE)
    return gate_norm(retained, gate)

def block_total(term, count):
    total = None
    for block in range(count):
        part = lax.optimization_barrier(term(block).astype(jnp.bfloat16)).astype(jnp.float32)
        total = part if total is None else total + part
    return total

def reference(inputs, first_gain, first_shift, query_weight, key_weight, value_weight, gate_weight, output_weight, second_gain, second_shift, inner_weight, inner_bias, outer_weight, outer_bias, cotangent, lengths, owners, offsets):
    key_width = HEADS * DK // N_TENSOR
    value_width = HEADS * DV // N_TENSOR
    hidden_width = FF // N_TENSOR
    log_decay = head_decay(0, HEADS)
    slots = jnp.arange(TOKEN_SLOTS_EACH, dtype=jnp.int32)
    ends = offsets + lengths

    def group_pass(carry, item):
        group, tokens, incoming = item
        inside = (owners[None, :] == group) & (offsets[None, :] <= slots[:, None]) & (slots[:, None] < ends[None, :])
        valid = jnp.any(inside, axis=1)
        starts = (lax.optimization_barrier(jnp.sum(jnp.where(inside, offsets[None, :], 0), axis=1)) + jnp.where(valid, 0, slots)).astype(jnp.int32)
        live = valid[:, None]

        def mixer(query, keys, values, gate):
            return retention_whole(query, keys, values, gate, starts, log_decay)
        tokens_wide = tokens.astype(jnp.float32)
        normed_one, first_back = jax.vjp(layer_norm, tokens_wide, first_gain, first_shift)
        act_one = normed_one.astype(jnp.bfloat16)
        query = product(act_one, query_weight)
        keys = product(act_one, key_weight)
        values = product(act_one, value_weight)
        gate = product(act_one, gate_weight)
        mixed, mix_back = jax.vjp(mixer, query, keys, values, gate)
        mixed_low = mixed.astype(jnp.bfloat16)

        def attn_term(block):
            window = slice(block * value_width, (block + 1) * value_width)
            return product(mixed_low[:, window], output_weight[window])
        resid = tokens_wide + block_total(attn_term, N_TENSOR)
        normed_two, second_back = jax.vjp(layer_norm, resid, second_gain, second_shift)
        act_two = normed_two.astype(jnp.bfloat16)
        preact = product(act_two, inner_weight) + inner_bias
        hidden, gelu_back = jax.vjp(gelu_exact, preact)
        hidden_low = hidden.astype(jnp.bfloat16)

        def ffn_term(block):
            window = slice(block * hidden_width, (block + 1) * hidden_width)
            return product(hidden_low[:, window], outer_weight[window])
        feedforward = block_total(ffn_term, N_TENSOR)
        outputs = jnp.where(live, resid + feedforward + outer_bias, 0.0).astype(jnp.bfloat16)
        grad_out = jnp.where(live, incoming.astype(jnp.float32), 0.0)
        grad_out_low = grad_out.astype(jnp.bfloat16)
        outer_bias_grad = lax.optimization_barrier(jnp.sum(grad_out, axis=0))
        outer_grad = product(hidden_low.T, grad_out_low)
        grad_pre, = gelu_back(product(grad_out_low, outer_weight.T))
        grad_pre_low = grad_pre.astype(jnp.bfloat16)
        inner_bias_grad = lax.optimization_barrier(jnp.sum(grad_pre, axis=0))
        inner_grad = product(act_two.T, grad_pre_low)

        def ffn_back_term(block):
            window = slice(block * hidden_width, (block + 1) * hidden_width)
            return product(grad_pre_low[:, window], inner_weight[:, window].T)
        grad_act_two = block_total(ffn_back_term, N_TENSOR)
        grad_resid_norm, second_gain_grad, second_shift_grad = second_back(grad_act_two)
        grad_resid = grad_out + grad_resid_norm
        grad_resid_low = grad_resid.astype(jnp.bfloat16)
        output_grad = product(mixed_low.T, grad_resid_low)
        grad_query, grad_keys, grad_values, grad_gate = mix_back(product(grad_resid_low, output_weight.T))
        query_low = grad_query.astype(jnp.bfloat16)
        keys_low = grad_keys.astype(jnp.bfloat16)
        values_low = grad_values.astype(jnp.bfloat16)
        gate_low = grad_gate.astype(jnp.bfloat16)
        query_grad = product(act_one.T, query_low)
        key_grad = product(act_one.T, keys_low)
        value_grad = product(act_one.T, values_low)
        gate_grad = product(act_one.T, gate_low)

        def attn_back_term(block):
            narrow = slice(block * key_width, (block + 1) * key_width)
            window = slice(block * value_width, (block + 1) * value_width)
            total = product(query_low[:, narrow], query_weight[:, narrow].T)
            total = total + product(keys_low[:, narrow], key_weight[:, narrow].T)
            total = total + product(values_low[:, window], value_weight[:, window].T)
            return total + product(gate_low[:, window], gate_weight[:, window].T)
        grad_act_one = block_total(attn_back_term, N_TENSOR)
        grad_in_norm, first_gain_grad, first_shift_grad = first_back(grad_act_one)
        input_grad = grad_resid + grad_in_norm
        grads = (first_gain_grad, first_shift_grad, query_grad, key_grad, value_grad, gate_grad, output_grad, second_gain_grad, second_shift_grad, inner_grad, inner_bias_grad, outer_grad, outer_bias_grad)
        carry = jax.tree.map(lambda left, right: left + right, carry, grads)
        return (carry, (outputs, input_grad))
    start_grads = (jnp.zeros((D,), jnp.float32), jnp.zeros((D,), jnp.float32), jnp.zeros((D, HEADS * DK), jnp.float32), jnp.zeros((D, HEADS * DK), jnp.float32), jnp.zeros((D, HEADS * DV), jnp.float32), jnp.zeros((D, HEADS * DV), jnp.float32), jnp.zeros((HEADS * DV, D), jnp.float32), jnp.zeros((D,), jnp.float32), jnp.zeros((D,), jnp.float32), jnp.zeros((D, FF), jnp.float32), jnp.zeros((FF,), jnp.float32), jnp.zeros((FF, D), jnp.float32), jnp.zeros((D,), jnp.float32))
    items = (jnp.arange(N_DP, dtype=jnp.int32), inputs.reshape(N_DP, TOKEN_SLOTS_EACH, D), cotangent.reshape(N_DP, TOKEN_SLOTS_EACH, D))
    final, (outputs, input_grad) = lax.scan(group_pass, start_grads, items)
    first_gain_grad, first_shift_grad, query_grad, key_grad, value_grad, gate_grad, output_grad, second_gain_grad, second_shift_grad, inner_grad, inner_bias_grad, outer_grad, outer_bias_grad = final
    return (outputs.reshape(TOKENS, D), input_grad.reshape(TOKENS, D), first_gain_grad, first_shift_grad, query_grad, key_grad, value_grad, gate_grad, output_grad, second_gain_grad, second_shift_grad, inner_grad, inner_bias_grad, outer_grad, outer_bias_grad)
```

```python
import functools

import jax
import jax.numpy as jnp
from jax import lax
from jax.experimental import pallas as pl
from jax.experimental.pallas import tpu as pltpu
from jax.sharding import PartitionSpec as P

HEADS = 8
EPS = 1e-05
F32 = jnp.float32
BF16 = jnp.bfloat16
NN = (((1,), (0,)), ((), ()))
NT = (((1,), (1,)), ((), ()))
TN = (((0,), (0,)), ((), ()))
VMEM_LIMIT = 60 * 1024 * 1024


def mm(left, right, dims):
    return lax.dot_general(left, right, dims, preferred_element_type=F32)


def mm_low(left, right, dims):
    return mm(left.astype(BF16), right.astype(BF16), dims)


def mm_high(left, right, dims):
    left_top, right_top = left.astype(BF16), right.astype(BF16)
    left_rest = (left - left_top.astype(F32)).astype(BF16)
    right_rest = (right - right_top.astype(F32)).astype(BF16)
    small = mm(left_top, right_rest, dims) + mm(left_rest, right_top, dims)
    return small + mm(left_top, right_top, dims)


def head_decay(first_head, count):
    heads = (first_head + jnp.arange(count, dtype=jnp.int32)).astype(F32)
    return jnp.log1p(-jnp.exp2(-5.0 - heads))


def cost(flops, bytes_accessed):
    return pl.CostEstimate(flops=int(flops), bytes_accessed=int(bytes_accessed), transcendentals=0)


def params():
    return pltpu.CompilerParams(vmem_limit_bytes=VMEM_LIMIT)


def whole(shape):
    zeros = (0,) * len(shape)
    return pl.BlockSpec(shape, lambda *_: zeros)


def decay_weights(start, lam):
    rows = start.shape[0]
    row = lax.broadcasted_iota(jnp.int32, (rows, rows), 0)
    col = lax.broadcasted_iota(jnp.int32, (rows, rows), 1)
    live = (col <= row) & (col >= start)
    power = jnp.where(live, (row - col).astype(F32) * lam, 0.0)
    return jnp.where(live, jnp.exp(power), 0.0)


def normalize(value, eps):
    center = value - jnp.mean(value, axis=-1, keepdims=True)
    spread = jnp.mean(center * center, axis=-1, keepdims=True)
    inverse = lax.rsqrt(spread + eps)
    return center * inverse, inverse


def norm_back(hat, inverse, grad):
    return inverse * (
        grad
        - jnp.mean(grad, axis=-1, keepdims=True)
        - hat * jnp.mean(grad * hat, axis=-1, keepdims=True)
    )


def split_heads(block, dk, dv):
    return (
        block[:, :dk],
        block[:, dk : 2 * dk],
        block[:, 2 * dk : 2 * dk + dv],
        block[:, 2 * dk + dv :],
    )


def emit_pieces(total, tensor_index, outs):
    rows = outs[0].shape[0]
    for step, out in enumerate(outs):
        place = pl.multiple_of((tensor_index ^ step) * rows, rows)
        out[...] = total[pl.ds(place, rows), :].astype(out.dtype)


def join_pieces(pieces, tensor_index, full):
    rows = pieces[0].shape[-2]
    for step, piece in enumerate(pieces):
        place = pl.multiple_of((tensor_index ^ step) * rows, rows)
        full[pl.ds(place, rows), :] = piece[...].reshape(rows, full.shape[1])


def project_kernel(chain, count, dk, dv, lam_ref, place_ref, *refs):
    xs, refs = refs[:count], refs[count:]
    if chain:
        gain, shift, wq, wk, wv, wg, start, wo, act, wide = refs[:10]
        outs, total = refs[10:-1], refs[-1]
    else:
        gain, shift, wq, wk, wv, wg, act, wide = refs
    head = pl.program_id(0)

    @pl.when(head == 0)
    def _():
        rows = xs[0].shape[0]
        for k, x in enumerate(xs):
            hat, _ = normalize(x[...].astype(F32), EPS)
            act[k * rows : (k + 1) * rows, :] = (hat * gain[...] + shift[...]).astype(BF16)

    query = mm(act[...], wq[...], NN)
    wide[:, :dk] = query
    keys = mm(act[...], wk[...], NN)
    wide[:, dk : 2 * dk] = keys
    values = mm(act[...], wv[...], NN)
    wide[:, 2 * dk : 2 * dk + dv] = values
    gate = mm(act[...], wg[...], NN)
    wide[:, 2 * dk + dv :] = gate
    if chain:
        weight = decay_weights(start[0], lam_ref[head])
        scores = mm_high(query, keys, NT) * weight
        hat, _ = normalize(mm_high(scores, values, NN), 1.0)
        mixed = (gate / (1.0 + jnp.exp(-gate)) * hat).astype(BF16)
        term = mm(mixed, wo[...], NN)

        @pl.when(head == 0)
        def _():
            total[...] = term

        @pl.when(head > 0)
        def _():
            total[...] += term

        @pl.when(head == pl.num_programs(0) - 1)
        def _():
            emit_pieces(total, place_ref[0], outs)


def project(chain, xs, gain, shift, wq, wk, wv, wg, lam, place, starts, wo, n_t):
    count = len(xs)
    rows, width = xs[0].shape
    heads = lam.shape[0]
    dk, dv = wq.shape[1] // heads, wv.shape[1] // heads
    span = 2 * dk + 2 * dv
    cols = lambda size: pl.BlockSpec((width, size), lambda h, *_: (0, h))
    in_specs = [whole((rows, width))] * count + [
        whole((1, width)),
        whole((1, width)),
        cols(dk),
        cols(dk),
        cols(dv),
        cols(dv),
    ]
    operands = [*xs, gain, shift, wq, wk, wv, wg]
    out_specs = [
        whole((count * rows, width)),
        pl.BlockSpec((count * rows, span), lambda h, *_: (0, h)),
    ]
    out_shape = [
        jax.ShapeDtypeStruct((count * rows, width), BF16),
        jax.ShapeDtypeStruct((count * rows, heads * span), F32),
    ]
    scratch = []
    if chain:
        in_specs += [
            pl.BlockSpec((1, rows, 1), lambda h, *_: (0, 0, 0)),
            pl.BlockSpec((dv, width), lambda h, *_: (h, 0)),
        ]
        operands += [starts, wo]
        out_specs += [whole((rows // n_t, width))] * n_t
        out_shape += [jax.ShapeDtypeStruct((rows // n_t, width), BF16)] * n_t
        scratch = [pltpu.VMEM((rows, width), F32)]
    flops = 2 * count * rows * width * span * heads
    return pl.pallas_call(
        functools.partial(project_kernel, chain, count, dk, dv),
        grid_spec=pltpu.PrefetchScalarGridSpec(
            num_scalar_prefetch=2,
            grid=(heads,),
            in_specs=in_specs,
            out_specs=out_specs,
            scratch_shapes=scratch,
        ),
        out_shape=out_shape,
        compiler_params=params(),
        cost_estimate=cost(flops * 1.6, width * span * heads * 2 + count * rows * span * heads * 4),
        name="project_chain" if chain else "project_other",
    )(lam, place, *operands)


def retention_back_kernel(chain, count, rows, dk, dv, n_t, lam_ref, place_ref, *refs):
    wide, start, wo = refs[:3]
    pieces = refs[3 : 3 + n_t]
    rest = refs[3 + n_t :]
    if chain:
        wq, wk, wv, wg, grad_full, low, mixed_out = rest[:7]
        outs, total = rest[7:-1], rest[-1]
    else:
        grad_full, low, mixed_out = rest
    head = pl.program_id(0)

    @pl.when(head == 0)
    def _():
        for k in range(count):
            join_pieces(
                [piece.at[k] for piece in pieces],
                place_ref[0],
                grad_full.at[k * rows : (k + 1) * rows, :],
            )

    for k in range(count):
        span = slice(k * rows, (k + 1) * rows)
        query, keys, values, gate = split_heads(wide[span, :], dk, dv)
        weight = decay_weights(start[k], lam_ref[head])
        scores = mm_high(query, keys, NT) * weight
        hat, inverse = normalize(mm_high(scores, values, NN), 1.0)
        sig = 1.0 / (1.0 + jnp.exp(-gate))
        silu = gate * sig
        mixed_out[span, :] = (silu * hat).astype(BF16)
        grad_mixed = mm(grad_full[span, :], wo[...], NT)
        gate_low = (grad_mixed * hat * (sig * (1.0 + gate * (1.0 - sig)))).astype(BF16)
        grad_kept = norm_back(hat, inverse, grad_mixed * silu)
        grad_scores = mm_high(grad_kept, values, NT) * weight
        values_low = mm_low(scores, grad_kept, TN).astype(BF16)
        query_low = mm_low(grad_scores, keys, NN).astype(BF16)
        keys_low = mm_low(grad_scores, query, TN).astype(BF16)
        low[span, :dk] = query_low
        low[span, dk : 2 * dk] = keys_low
        low[span, 2 * dk : 2 * dk + dv] = values_low
        low[span, 2 * dk + dv :] = gate_low
    if chain:
        term = mm(query_low, wq[...], NT) + mm(keys_low, wk[...], NT)
        term = term + mm(values_low, wv[...], NT) + mm(gate_low, wg[...], NT)

        @pl.when(head == 0)
        def _():
            total[...] = term

        @pl.when(head > 0)
        def _():
            total[...] += term

        @pl.when(head == pl.num_programs(0) - 1)
        def _():
            emit_pieces(total, place_ref[0], outs)


def retention_back(chain, wide, starts, wo, pieces, weights, lam, place, n_t):
    count, rows = starts.shape[:2]
    width = wo.shape[1]
    heads = lam.shape[0]
    wq, wk, wv, wg = weights
    dk, dv = wq.shape[1] // heads, wv.shape[1] // heads
    span = 2 * dk + 2 * dv
    cols = lambda size: pl.BlockSpec((width, size), lambda h, *_: (0, h))
    in_specs = [
        pl.BlockSpec((count * rows, span), lambda h, *_: (0, h)),
        whole((count, rows, 1)),
        pl.BlockSpec((dv, width), lambda h, *_: (h, 0)),
    ] + [whole((count, rows // n_t, width))] * n_t
    operands = [wide, starts, wo, *pieces]
    out_specs = [
        whole((count * rows, width)),
        pl.BlockSpec((count * rows, span), lambda h, *_: (0, h)),
        pl.BlockSpec((count * rows, dv), lambda h, *_: (0, h)),
    ]
    out_shape = [
        jax.ShapeDtypeStruct((count * rows, width), BF16),
        jax.ShapeDtypeStruct((count * rows, heads * span), BF16),
        jax.ShapeDtypeStruct((count * rows, heads * dv), BF16),
    ]
    scratch = []
    flops = count * (2 * rows * width * dv * heads + 30 * rows * rows * dv * heads * 2)
    if chain:
        in_specs += [cols(dk), cols(dk), cols(dv), cols(dv)]
        operands += [wq, wk, wv, wg]
        out_specs += [whole((rows // n_t, width))] * n_t
        out_shape += [jax.ShapeDtypeStruct((rows // n_t, width), BF16)] * n_t
        scratch = [pltpu.VMEM((rows, width), F32)]
        flops += 2 * rows * width * span * heads
    return pl.pallas_call(
        functools.partial(retention_back_kernel, chain, count, rows, dk, dv, n_t),
        grid_spec=pltpu.PrefetchScalarGridSpec(
            num_scalar_prefetch=2,
            grid=(heads,),
            in_specs=in_specs,
            out_specs=out_specs,
            scratch_shapes=scratch,
        ),
        out_shape=out_shape,
        compiler_params=params(),
        cost_estimate=cost(flops * 2, count * rows * span * heads * 6 + heads * dv * width * 2),
        name="mix_back_chain" if chain else "mix_back_other",
    )(lam, place, *operands)


def feed_kernel(chain, count, rows, n_t, place_ref, *refs):
    cots, refs = refs[:count], refs[count:]
    valid, inner, bias, outer = refs[:4]
    pieces = refs[4 : 4 + n_t]
    rest = refs[4 + n_t :]
    act, hidden_out, grad_out, bias_sum, out_sum = rest[:5]
    step = pl.program_id(0)

    @pl.when(step == 0)
    def _():
        for k in range(count):
            join_pieces(
                [piece.at[k] for piece in pieces],
                place_ref[0],
                act.at[k * rows : (k + 1) * rows, :],
            )
            kept = jnp.where(valid[k] > 0, cots[k][...].astype(F32), 0.0)
            out_sum[k : k + 1, :] = jnp.sum(kept, axis=0, keepdims=True)

    for k in range(count):
        span = slice(k * rows, (k + 1) * rows)
        live = valid[k] > 0
        preact = mm(act[span, :], inner[...], NN) + bias[...]
        grad = jnp.where(live, mm(cots[k][...], outer[...], NT), 0.0)
        cdf = 0.5 * (1.0 + lax.erf(preact * 0.7071067811865476))
        slope = cdf + preact * (jnp.exp(-0.5 * preact * preact) * 0.3989422804014327)
        hidden = jnp.where(live, preact * cdf, 0.0).astype(BF16)
        grad_pre = grad * slope
        bias_sum[k : k + 1, :] = jnp.sum(grad_pre, axis=0, keepdims=True)
        grad_low = grad_pre.astype(BF16)
        hidden_out[span, :] = hidden
        grad_out[span, :] = grad_low
    if chain:
        outs_two = rest[5 : 5 + n_t]
        outs_three = rest[5 + n_t : 5 + 2 * n_t]
        total_two, total_three = rest[-2:]
        term_two = mm(hidden, outer[...], NN)
        term_three = mm(grad_low, inner[...], NT)

        @pl.when(step == 0)
        def _():
            total_two[...] = term_two
            total_three[...] = term_three

        @pl.when(step > 0)
        def _():
            total_two[...] += term_two
            total_three[...] += term_three

        @pl.when(step == pl.num_programs(0) - 1)
        def _():
            emit_pieces(total_three, place_ref[0], outs_three)
            emit_pieces(total_two, place_ref[0], outs_two)


def feed(chain, cots, valid, inner, bias, outer, pieces, place, n_t):
    count, rows = valid.shape[:2]
    width, ff = inner.shape
    chunk = min(256, ff)
    in_specs = [whole((rows, width))] * count + [
        whole((count, rows, 1)),
        pl.BlockSpec((width, chunk), lambda i, *_: (0, i)),
        pl.BlockSpec((1, chunk), lambda i, *_: (0, i)),
        pl.BlockSpec((chunk, width), lambda i, *_: (i, 0)),
    ] + [whole((count, rows // n_t, width))] * n_t
    out_specs = [
        whole((count * rows, width)),
        pl.BlockSpec((count * rows, chunk), lambda i, *_: (0, i)),
        pl.BlockSpec((count * rows, chunk), lambda i, *_: (0, i)),
        pl.BlockSpec((count, chunk), lambda i, *_: (0, i)),
        whole((count, width)),
    ]
    out_shape = [
        jax.ShapeDtypeStruct((count * rows, width), BF16),
        jax.ShapeDtypeStruct((count * rows, ff), BF16),
        jax.ShapeDtypeStruct((count * rows, ff), BF16),
        jax.ShapeDtypeStruct((count, ff), F32),
        jax.ShapeDtypeStruct((count, width), F32),
    ]
    scratch = []
    flops = 4 * count * rows * width * ff
    if chain:
        out_specs += [whole((rows // n_t, width))] * (2 * n_t)
        out_shape += [jax.ShapeDtypeStruct((rows // n_t, width), BF16)] * (2 * n_t)
        scratch = [pltpu.VMEM((rows, width), F32)] * 2
        flops *= 2
    return pl.pallas_call(
        functools.partial(feed_kernel, chain, count, rows, n_t),
        grid_spec=pltpu.PrefetchScalarGridSpec(
            num_scalar_prefetch=1,
            grid=(ff // chunk,),
            in_specs=in_specs,
            out_specs=out_specs,
            scratch_shapes=scratch,
        ),
        out_shape=out_shape,
        compiler_params=params(),
        cost_estimate=cost(flops * 1.3, 4 * width * ff),
        name="feed_chain" if chain else "feed_other",
    )(place, *cots, valid, inner, bias, outer, *pieces)


def norm_two_kernel(n_t, place_ref, x, gain, shift, *refs):
    pieces, (resid, act) = refs[:n_t], refs[n_t:]
    total = pieces[0][...].astype(F32)
    for piece in pieces[1:]:
        total = total + piece[...].astype(F32)
    value = x[...].astype(F32) + total
    resid[...] = value
    hat, _ = normalize(value, EPS)
    act[...] = (hat * gain[...] + shift[...]).astype(BF16)


def norm_two(x, gain, shift, pieces, place):
    n_t = len(pieces)
    rows, width = pieces[0].shape
    return pl.pallas_call(
        functools.partial(norm_two_kernel, n_t),
        grid_spec=pltpu.PrefetchScalarGridSpec(
            num_scalar_prefetch=1,
            grid=(1,),
            in_specs=[
                pl.BlockSpec((rows, width), lambda i, place: (place[0], 0)),
                whole((1, width)),
                whole((1, width)),
            ]
            + [whole((rows, width))] * n_t,
            out_specs=[whole((rows, width))] * 2,
        ),
        out_shape=[
            jax.ShapeDtypeStruct((rows, width), F32),
            jax.ShapeDtypeStruct((rows, width), BF16),
        ],
        compiler_params=params(),
        cost_estimate=cost(rows * width * 20, rows * width * 16),
        name="norm_two",
    )(place, x, gain, shift, *pieces)


def norm_two_back_kernel(n_t, place_ref, cot, valid, gain, resid, *refs):
    pieces, (low, sums) = refs[:n_t], refs[n_t:]
    grad = pieces[0][...].astype(F32)
    for piece in pieces[1:]:
        grad = grad + piece[...].astype(F32)
    grad = grad.astype(BF16).astype(F32)
    hat, inverse = normalize(resid[...], EPS)
    sums[0:1, :] = jnp.sum(grad * hat, axis=0, keepdims=True)
    sums[1:2, :] = jnp.sum(grad, axis=0, keepdims=True)
    kept = jnp.where(valid[0] > 0, cot[...].astype(F32), 0.0)
    low[...] = (kept + norm_back(hat, inverse, grad * gain[...])).astype(BF16)


def norm_two_back(cot, valid, gain, resid, pieces, place):
    n_t = len(pieces)
    rows, width = resid.shape
    return pl.pallas_call(
        functools.partial(norm_two_back_kernel, n_t),
        grid_spec=pltpu.PrefetchScalarGridSpec(
            num_scalar_prefetch=1,
            grid=(1,),
            in_specs=[
                pl.BlockSpec((rows, width), lambda i, place: (place[0], 0)),
                pl.BlockSpec((1, rows, 1), lambda i, place: (0, place[0], 0)),
                whole((1, width)),
                whole((rows, width)),
            ]
            + [whole((rows, width))] * n_t,
            out_specs=[whole((rows, width)), whole((2, width))],
        ),
        out_shape=[
            jax.ShapeDtypeStruct((rows, width), BF16),
            jax.ShapeDtypeStruct((2, width), F32),
        ],
        compiler_params=params(),
        cost_estimate=cost(rows * width * 30, rows * width * 18),
        name="norm_two_back",
    )(place, cot, valid, gain, resid, *pieces)


def output_kernel(n_t, place_ref, valid, bias, resid, *refs):
    pieces, (out,) = refs[:n_t], refs[n_t:]
    total = pieces[0][...].astype(F32)
    for piece in pieces[1:]:
        total = total + piece[...].astype(F32)
    out[...] = jnp.where(valid[0] > 0, resid[...] + total + bias[...], 0.0).astype(BF16)


def output_rows(valid, bias, resid, pieces, place):
    n_t = len(pieces)
    rows, width = resid.shape
    return pl.pallas_call(
        functools.partial(output_kernel, n_t),
        grid_spec=pltpu.PrefetchScalarGridSpec(
            num_scalar_prefetch=1,
            grid=(1,),
            in_specs=[
                pl.BlockSpec((1, rows, 1), lambda i, place: (0, place[0], 0)),
                whole((1, width)),
                whole((rows, width)),
            ]
            + [whole((rows, width))] * n_t,
            out_specs=whole((rows, width)),
        ),
        out_shape=jax.ShapeDtypeStruct((rows, width), BF16),
        compiler_params=params(),
        cost_estimate=cost(rows * width * 10, rows * width * 14),
        name="output_rows",
    )(place, valid, bias, resid, *pieces)


def sum_kernel(*refs):
    pieces, out = refs[:-1], refs[-1]
    total = pieces[0][...].astype(F32)
    for piece in pieces[1:]:
        total = total + piece[...].astype(F32)
    out[...] = total.astype(out.dtype)


def sum_pieces(pieces):
    return pl.pallas_call(
        sum_kernel,
        out_shape=jax.ShapeDtypeStruct(pieces[0].shape, BF16),
        compiler_params=params(),
        cost_estimate=cost(pieces[0].size * 4, pieces[0].size * 10),
        name="sum_pieces",
    )(*pieces)


def join_kernel(n_t, place_ref, *refs):
    join_pieces(refs[:n_t], place_ref[0], refs[n_t])


def join(pieces, place):
    n_t = len(pieces)
    rows, width = pieces[0].shape
    return pl.pallas_call(
        functools.partial(join_kernel, n_t),
        grid_spec=pltpu.PrefetchScalarGridSpec(
            num_scalar_prefetch=1,
            grid=(1,),
            in_specs=[whole((rows, width))] * n_t,
            out_specs=whole((rows * n_t, width)),
        ),
        out_shape=jax.ShapeDtypeStruct((rows * n_t, width), pieces[0].dtype),
        compiler_params=params(),
        cost_estimate=cost(rows * width, rows * width * 16),
        name="join_rows",
    )(place, *pieces)


def norm_one_back_kernel(n_t, place_ref, x, gain, grad_resid, *refs):
    pieces, (out, sums, full) = refs[:n_t], refs[n_t:]
    join_pieces(pieces, place_ref[0], full)
    grad = full[...].astype(F32)
    hat, inverse = normalize(x[...].astype(F32), EPS)
    sums[0:1, :] = jnp.sum(grad * hat, axis=0, keepdims=True)
    sums[1:2, :] = jnp.sum(grad, axis=0, keepdims=True)
    out[...] = grad_resid[...].astype(F32) + norm_back(hat, inverse, grad * gain[...])


def norm_one_back(x, gain, grad_resid, pieces, place):
    n_t = len(pieces)
    rows, width = x.shape
    return pl.pallas_call(
        functools.partial(norm_one_back_kernel, n_t),
        grid_spec=pltpu.PrefetchScalarGridSpec(
            num_scalar_prefetch=1,
            grid=(1,),
            in_specs=[whole((rows, width)), whole((1, width)), whole((rows, width))]
            + [whole((rows // n_t, width))] * n_t,
            out_specs=[whole((rows, width)), whole((2, width))],
            scratch_shapes=[pltpu.VMEM((rows, width), BF16)],
        ),
        out_shape=[
            jax.ShapeDtypeStruct((rows, width), F32),
            jax.ShapeDtypeStruct((2, width), F32),
        ],
        compiler_params=params(),
        cost_estimate=cost(rows * width * 30, rows * width * 10),
        name="norm_one_back",
    )(place, x, gain, grad_resid, *pieces)


def weight_grad_kernel(count, rows, plan, *refs):
    lefts, rights, outs = refs[:count], refs[count : -plan[-1][0] - 1], refs[-plan[-1][0] - 1 :]

    def groups(sides):
        return [(side, k) for side in sides for k in range(0, side.shape[0], rows)]

    pairs = list(zip(groups(lefts), groups(rights)))
    for out, target, source, size in plan:
        parts = [
            mm(
                left[i : i + rows, :],
                right[j : j + rows, source : source + size],
                TN,
            )
            for (left, i), (right, j) in pairs
        ]
        while len(parts) > 1:
            parts = [parts[i] + parts[i + 1] for i in range(0, len(parts), 2)]
        outs[out][:, target : target + size] = parts[0]


def weight_grad(rows, lefts, rights, widths, plan, name):
    height = lefts[0].shape[1]
    tile = 256
    total = sum(widths)
    depth = sum(left.shape[0] for left in lefts)
    return pl.pallas_call(
        functools.partial(weight_grad_kernel, len(lefts), rows, plan),
        grid=(height // tile,),
        in_specs=[pl.BlockSpec((left.shape[0], tile), lambda i: (0, i)) for left in lefts]
        + [
            pl.BlockSpec(right.shape, lambda i: (0, 0), pipeline_mode=pl.Buffered(1))
            for right in rights
        ],
        out_specs=[pl.BlockSpec((tile, w), lambda i: (i, 0)) for w in widths],
        out_shape=[jax.ShapeDtypeStruct((height, w), F32) for w in widths],
        compiler_params=params(),
        cost_estimate=cost(2 * depth * height * total, 4 * height * total),
        name=name,
    )(*lefts, *rights)


def plain_plan(width):
    size = min(512, width)
    return [(0, c, c, size) for c in range(0, width, size)]


def head_plan(heads, dk, dv):
    plan = []
    for head in range(heads):
        base = head * (2 * dk + 2 * dv)
        plan.append((0, head * dk, base, dk))
        plan.append((1, head * dk, base + dk, dk))
        plan.append((2, head * dv, base + 2 * dk, dv))
        plan.append((3, head * dv, base + 2 * dk + dv, dv))
    return plan


def shards(
    inputs,
    first_gain,
    first_shift,
    query_weight,
    key_weight,
    value_weight,
    gate_weight,
    output_weight,
    second_gain,
    second_shift,
    inner_weight,
    inner_bias,
    outer_weight,
    outer_bias,
    cotangent,
    lengths,
    owners,
    offsets,
):
    rows, width = inputs.shape
    n_t = lax.axis_size("tensor")
    n_dp = lax.axis_size("dp")
    n_z = n_dp // 2
    heads = HEADS // n_t
    dk = query_weight.shape[1] // heads
    dv = value_weight.shape[1] // heads
    group = lax.axis_index("dp")
    tensor = lax.axis_index("tensor")
    place = tensor.astype(jnp.int32).reshape(1)
    lam = head_decay(tensor * heads, heads)

    def swap_dp(value, step):
        return lax.ppermute(value, "dp", [(i, i ^ step) for i in range(n_dp)])

    def swap_t(value, step):
        return lax.ppermute(value, "tensor", [(i, i ^ step) for i in range(n_t)])

    def scatter(pieces):
        return [pieces[0]] + [swap_t(pieces[s], s) for s in range(1, n_t)]

    def spread(piece):
        return [piece] + [swap_t(piece, s) for s in range(1, n_t)]

    groups = group ^ (2 * jnp.arange(n_z, dtype=jnp.int32))
    slots = jnp.arange(rows, dtype=jnp.int32)
    ends = offsets + lengths
    inside = (
        (owners[None, None, :] == groups[:, None, None])
        & (offsets[None, None, :] <= slots[None, :, None])
        & (slots[None, :, None] < ends[None, None, :])
    )
    valid = jnp.any(inside, axis=2)
    starts = jnp.sum(jnp.where(inside, offsets[None, None, :], 0), axis=2) + jnp.where(
        valid, 0, slots[None, :]
    )
    starts = starts.astype(jnp.int32)[:, :, None]
    valid = valid.astype(jnp.int32)[:, :, None]

    gain_one, shift_one = first_gain[None, :], first_shift[None, :]
    gain_two, shift_two = second_gain[None, :], second_shift[None, :]
    bias_in, bias_out = inner_bias[None, :], outer_bias[None, :]
    weights = (query_weight, key_weight, value_weight, gate_weight)

    def scope(name):
        return jax.named_scope(name)

    def stack_others(piece, name):
        with scope(name + "_z"):
            parts = [swap_dp(piece, 2 * k) for k in range(1, n_z)]
        with scope(name + "_stack"):
            parts = jnp.stack(parts)
        with scope(name + "_t"):
            return spread(parts)

    with scope("gather_x"):
        xs = [swap_dp(inputs, 2 * k) for k in range(1, n_z)]
    with scope("gather_c"):
        cots = [swap_dp(cotangent, 2 * k) for k in range(1, n_z)]

    act, wide, *out_pieces = project(
        True, [inputs], gain_one, shift_one, *weights, lam, place, starts, output_weight, n_t
    )
    with scope("sum_one"):
        out_pieces = scatter(out_pieces)
    resid, act_two = norm_two(inputs, gain_two, shift_two, out_pieces, place)
    with scope("spread_two"):
        pieces = [piece[None] for piece in spread(act_two)]
    act_full, hidden, grad_pre, bias_sum, out_sum, *more = feed(
        True, [cotangent], valid[:1], inner_weight, bias_in, outer_weight, pieces, place, n_t
    )
    with scope("sum_three"):
        back_three = scatter(more[n_t:])
    resid_low, second_sums = norm_two_back(
        cotangent, valid, gain_two, resid, back_three, place
    )
    with scope("spread_three"):
        pieces = [piece[None] for piece in spread(resid_low)]
    grad_full, low, mixed, *back_pieces = retention_back(
        True, wide, starts[:1], output_weight, pieces, weights, lam, place, n_t
    )
    with scope("sum_four"):
        back_pieces = sum_pieces(scatter(back_pieces))
    with scope("spread_four"):
        grad_one = spread(back_pieces)
    input_grad, first_sums = norm_one_back(inputs, gain_one, grad_full, grad_one, place)

    with scope("sum_two"):
        forward_two = scatter(more[:n_t])
    outputs = output_rows(valid, bias_out, resid, forward_two, place)
    with scope("spread_out"):
        outputs = spread(outputs)
    outputs = join(outputs, place)

    act_other, wide_other = project(
        False, xs, gain_one, shift_one, *weights, lam, place, None, None, n_t
    )
    act_full_other, hidden_other, grad_pre_other, bias_other, out_other = feed(
        False,
        cots,
        valid[1:],
        inner_weight,
        bias_in,
        outer_weight,
        stack_others(act_two, "second"),
        place,
        n_t,
    )
    grad_full_other, low_other, mixed_other = retention_back(
        False,
        wide_other,
        starts[1:],
        output_weight,
        stack_others(resid_low, "third"),
        weights,
        lam,
        place,
        n_t,
    )

    def both(*values):
        return [*values, *[swap_dp(value, 1) for value in values]]

    (inner_grad,) = weight_grad(
        rows,
        both(act_full, act_full_other),
        both(grad_pre, grad_pre_other),
        (inner_weight.shape[1],),
        plain_plan(inner_weight.shape[1]),
        "inner_grad",
    )
    (outer_grad,) = weight_grad(
        rows,
        both(hidden, hidden_other),
        both(cotangent, *cots),
        (width,),
        plain_plan(width),
        "outer_grad",
    )
    (output_grad,) = weight_grad(
        rows,
        both(mixed, mixed_other),
        both(grad_full, grad_full_other),
        (width,),
        plain_plan(width),
        "output_grad",
    )
    query_grad, key_grad, value_grad, gate_grad = weight_grad(
        rows,
        both(act, act_other),
        both(low, low_other),
        tuple(w.shape[1] for w in weights),
        head_plan(heads, dk, dv),
        "qkvg_grad",
    )

    def butterfly(value, axis, size, first):
        step = first
        while step < size:
            value = value + lax.ppermute(value, axis, [(i, i ^ step) for i in range(size)])
            step *= 2
        return value

    def group_sum(own, other):
        values = [own] + [other[k : k + 1] for k in range(n_z - 1)]
        while len(values) > 1:
            values = [values[i] + values[i + 1] for i in range(0, len(values), 2)]
        return values[0]

    inner_bias_grad = group_sum(bias_sum, bias_other)
    inner_bias_grad = (inner_bias_grad + swap_dp(inner_bias_grad, 1))[0]
    outer_bias_grad = group_sum(out_sum, out_other)
    outer_bias_grad = (outer_bias_grad + swap_dp(outer_bias_grad, 1))[0]
    second_sums = butterfly(second_sums, "tensor", n_t, 1)
    sums = butterfly(jnp.concatenate([first_sums, second_sums]), "dp", n_dp, 1)
    first_sums, second_sums = sums[:2], sums[2:]
    return (
        outputs,
        input_grad,
        first_sums[0],
        first_sums[1],
        query_grad,
        key_grad,
        value_grad,
        gate_grad,
        output_grad,
        second_sums[0],
        second_sums[1],
        inner_grad,
        inner_bias_grad,
        outer_grad,
        outer_bias_grad,
    )


def solution(mesh):
    return jax.shard_map(
        shards,
        mesh=mesh,
        in_specs=(
            P("dp", None),
            P(),
            P(),
            P(None, "tensor"),
            P(None, "tensor"),
            P(None, "tensor"),
            P(None, "tensor"),
            P("tensor", None),
            P(),
            P(),
            P(None, "tensor"),
            P("tensor"),
            P("tensor", None),
            P(),
            P("dp", None),
            P(),
            P(),
            P(),
        ),
        out_specs=(
            P("dp", None),
            P("dp", None),
            P(),
            P(),
            P(None, "tensor"),
            P(None, "tensor"),
            P(None, "tensor"),
            P(None, "tensor"),
            P("tensor", None),
            P(),
            P(),
            P(None, "tensor"),
            P("tensor"),
            P("tensor", None),
            P(),
        ),
        check_vma=False,
    )
```
